32 devices in a mesh: dp: 8 (over z, x), tensor: 4 (over y, core).
Axes of the slice: x: 2, y: 2, z: 4, core: 2. Of those that a mesh axis runs over, the one named last changes fastest.
Arguments:
- tokens: bfloat16 [4096, 1024], P(('dp', 'tensor')), may hold values from -6 to 6
- seg_starts: int32 [8, 6], P('dp'), may hold values from 1 to 511, as said below
- norm1_gain: float32 [1024], replicated, may hold values from 0.5 to 1.5
- w_mix: bfloat16 [1024, 8, 768], P(None, 'tensor'), may hold values from -0.1875 to 0.1875
- w_gates: bfloat16 [1024, 8, 2], P(None, 'tensor'), may hold values from -0.1875 to 0.1875
- conv_w: float32 [4, 8, 512], P(None, 'tensor'), may hold values from -3 to 3
- decay_rate: float32 [8], P('tensor'), may hold values from 0.001 to 0.1
- onorm_gain: float32 [8, 256], P('tensor'), may hold values from 0.5 to 1.5
- w_out: bfloat16 [8, 256, 1024], P('tensor'), may hold values from -0.25 to 0.25
- norm2_gain: float32 [1024], replicated, may hold values from 0.5 to 1.5
- w_gu: bfloat16 [1024, 2, 2816], P(None, None, 'tensor'), may hold values from -0.1875 to 0.1875
- w_down: bfloat16 [2816, 1024], P('tensor'), may hold values from -0.21875 to 0.21875
- cotangent: bfloat16 [4096, 1024], P(('dp', 'tensor')), may hold values from -6 to 6
Outputs:
- output: bfloat16 [4096, 1024], P(('dp', 'tensor'))
- grad_tokens: bfloat16 [4096, 1024], P(('dp', 'tensor'))
- grad_norm1_gain: float32 [1024], P('dp')
- grad_w_mix: float32 [1024, 8, 768], P('dp', 'tensor')
- grad_w_gates: float32 [1024, 8, 2], P('dp', 'tensor')
- grad_conv_w: float32 [4, 8, 512], P(None, 'tensor')
- grad_decay_rate: float32 [8], P('tensor')
- grad_onorm_gain: float32 [8, 256], P('tensor')
- grad_w_out: float32 [8, 256, 1024], P('tensor', None, 'dp')
- grad_norm2_gain: float32 [1024], P('dp')
- grad_w_gu: float32 [1024, 2, 2816], P('dp', None, 'tensor')
- grad_w_down: float32 [2816, 1024], P('tensor', 'dp')
The draws below stay inside these ranges and needn't reach their ends.
Inputs may be any that keep to these rules, and one draw needn't show every extreme that they name: `seg_starts`: each entry is a position where a document begins in that sequence; every row names one position twice.
All inputs are finite; a program needn't handle non-finite values.
Results may differ from the reference program's by a relative error of at most 0.024.
Values may be sent and summed in bfloat16 or wider, within the bound.
A program may use at most 128 MiB of HBM per device.

```python
import math
import jax
import jax.numpy as jnp
from jax import lax

D = 1024
H = 8
DV = 256
FF = 2816
LEN = 512
BLOCK = 64
NSTART = 6
MIX = 768
CONV = 512
SEQS = 8
TOKENS = 4096


def draw_seg_starts(key, part):
    score_key, row_key = jax.random.split(jax.random.fold_in(key, 17))
    scores = jax.random.randint(score_key, (SEQS, LEN - 1), 0, 2 ** 21)
    scores = scores * LEN + jnp.arange(LEN - 1, dtype=jnp.int32)[None, :]
    order = jnp.argsort(scores, axis=1)
    picked = (order[:, :NSTART] + 1).astype(jnp.int32)
    chosen_row = jax.random.randint(row_key, (), 0, SEQS)
    rows_idx = jnp.arange(SEQS, dtype=jnp.int32)[:, None]
    cols_idx = jnp.arange(NSTART, dtype=jnp.int32)[None, :]
    here = rows_idx == chosen_row
    picked = jnp.where(jnp.logical_and(here, cols_idx == 0), 1, picked)
    picked = jnp.where(jnp.logical_and(here, cols_idx == 1), LEN - 1, picked)
    picked = jnp.where(cols_idx == NSTART - 1, picked[:, :1], picked)
    return picked.astype(jnp.int32)


def level_of(stream_key, shape, cuts, low, top_value):
    level, own = 1.0, jax.random.fold_in(stream_key, 6)
    for dim, blocks in cuts:
        heights = jnp.exp(jax.random.uniform(jax.random.fold_in(own, dim), (blocks,), jnp.float32, low / len(cuts), top_value / len(cuts)))
        level = level * jnp.repeat(heights, shape[dim] // blocks).reshape([-1 if axis == dim else 1 for axis in range(len(shape))])
    return level


def normal_values(own_key, dims, deviation, bound, shards=(), kind=jnp.bfloat16):
    level = level_of(own_key, dims, shards, -0.22, 0.18) if shards else 1.0
    array = jax.random.normal(own_key, dims, jnp.float32) * deviation * level
    return jnp.minimum(jnp.maximum(array, -bound), bound).astype(kind)


def setup_inputs(seed: int = 0) -> dict:
    key_list = jax.random.split(jax.random.key(seed), 14)
    tokens = normal_values(key_list[0], (TOKENS, D), 1.0, 6.0, ((0, 32),))
    seg_starts = draw_seg_starts(jax.random.fold_in(key_list[13], 71), 0)
    norm1_gain = jnp.clip(1.0 + 0.1 * jax.random.normal(key_list[2], (D,), jnp.float32), 0.5, 1.5)
    w_mix = normal_values(key_list[3], (D, H, MIX), D ** -0.5, 0.1875, ((1, 4),))
    w_gates = normal_values(key_list[4], (D, H, 2), D ** -0.5, 0.1875, ((1, 4),))
    conv_w = normal_values(key_list[5], (4, H, CONV), 4 ** -0.5, 3.0, ((1, 4),), jnp.float32)
    decay_rate = jnp.clip(jnp.exp(math.log(0.1) - 4.6051702 * jax.random.uniform(key_list[6], (H,), jnp.float32) ** level_of(key_list[6], (H,), ((0, 4),), -0.2, 0.2)), 0.001, 0.1)
    onorm_gain = jnp.clip(1.0 + 0.1 * jax.random.normal(key_list[7], (H, DV), jnp.float32), 0.5, 1.5)
    w_out = normal_values(key_list[8], (H, DV, D), (H * DV // 4) ** -0.5, 0.25, ((0, 4),))
    norm2_gain = jnp.clip(1.0 + 0.1 * jax.random.normal(key_list[9], (D,), jnp.float32), 0.5, 1.5)
    w_gu = normal_values(key_list[10], (D, 2, FF), D ** -0.5, 0.1875, ((2, 4),))
    w_down = normal_values(key_list[11], (FF, D), (FF // 4) ** -0.5, 0.21875, ((0, 4),))
    cotangent = normal_values(key_list[12], (TOKENS, D), 1.0, 6.0, ((0, 32),))
    return dict(tokens=tokens, seg_starts=seg_starts, norm1_gain=norm1_gain, w_mix=w_mix, w_gates=w_gates, conv_w=conv_w, decay_rate=decay_rate, onorm_gain=onorm_gain, w_out=w_out, norm2_gain=norm2_gain, w_gu=w_gu, w_down=w_down, cotangent=cotangent)


def rms_norm(rows, gain):
    return rows * lax.rsqrt(lax.optimization_barrier(jnp.mean(rows * rows, axis=-1, keepdims=True)) + 1e-06) * gain

def segment_ids(starts_row, length):
    places = jnp.arange(length, dtype=jnp.int32)
    flags = jnp.any(starts_row[:, None] == places[None, :], axis=0).astype(jnp.int32)
    seg = jnp.cumsum(flags).astype(jnp.int32)
    before = jnp.concatenate([seg[:1], seg[:-1]])
    return (seg, before)

def core(proj, gates_pre, conv_w, decay_rate, onorm_gain, seg, before):
    highest = lax.Precision.HIGHEST
    length, heads, width = proj.shape
    value_width = onorm_gain.shape[-1]
    conv_cols = conv_w.shape[-1]
    key_width = (conv_cols - value_width) // 2
    mixed = proj[:, :, :conv_cols]
    total = jnp.zeros_like(mixed)
    for lag in range(4):
        moved = jnp.pad(mixed, ((lag, 0), (0, 0), (0, 0)))[:length]
        moved_seg = jnp.pad(seg, (lag, 0), constant_values=-1)[:length]
        keep = (moved_seg == seg).astype(jnp.float32)
        total = total + conv_w[3 - lag][None] * moved * keep[:, None, None]
    act = jax.nn.silu(total)
    query = act[..., :key_width]
    keys = act[..., key_width:2 * key_width]
    values = act[..., 2 * key_width:]
    query = query * lax.rsqrt(lax.optimization_barrier(jnp.sum(query * query, axis=-1, keepdims=True)) + 1e-06) * key_width ** (-0.5)
    keys = keys * lax.rsqrt(lax.optimization_barrier(jnp.sum(keys * keys, axis=-1, keepdims=True)) + 1e-06)
    gate_out = proj[..., conv_cols:]
    beta = jax.nn.sigmoid(gates_pre[..., 1])
    log_decay = -decay_rate[None, :] * jax.nn.softplus(gates_pre[..., 0])
    blocks = length // BLOCK

    def split(arr):
        return arr.reshape((blocks, BLOCK) + arr.shape[1:])
    items = (split(query), split(keys), split(values), split(beta), split(log_decay), split(seg), before.reshape(blocks, BLOCK)[:, 0])
    places = jnp.arange(BLOCK)
    inclusive = places[:, None] >= places[None, :]
    strict = (places[:, None] > places[None, :]).astype(jnp.float32)
    unit = jnp.eye(BLOCK, dtype=jnp.float32)

    def step(state, item):
        q_blk, k_blk, v_blk, beta_blk, logd_blk, seg_blk, prev = item
        cum = jnp.cumsum(logd_blk, axis=0)
        live = jnp.logical_and(seg_blk[:, None] == seg_blk[None, :], inclusive)
        diff = cum.T[:, :, None] - cum.T[:, None, :]
        within = jnp.exp(jnp.where(live[None], diff, 0.0)) * live[None].astype(jnp.float32)
        carried = jnp.exp(cum) * (seg_blk == prev).astype(jnp.float32)[:, None]
        kk = jnp.einsum('thd,jhd->htj', k_blk, k_blk, precision=highest)
        lower = beta_blk.T[:, :, None] * within * kk * strict[None]
        start_val = jnp.einsum('thd,hde->hte', k_blk, state, precision=highest)
        rhs = beta_blk.T[:, :, None] * (jnp.transpose(v_blk, (1, 0, 2)) - carried.T[:, :, None] * start_val)
        errs = lax.linalg.triangular_solve(unit[None] + lower, rhs, left_side=True, lower=True, unit_diagonal=True)
        qk = jnp.einsum('thd,jhd->htj', q_blk, k_blk, precision=highest)
        read = carried.T[:, :, None] * jnp.einsum('thd,hde->hte', q_blk, state, precision=highest)
        read = read + jnp.einsum('htj,hje->hte', within * qk, errs, precision=highest)
        final_row = within[:, -1, :]
        new_state = carried[-1][:, None, None] * state + jnp.einsum('hj,jhd,hje->hde', final_row, k_blk, errs, precision=highest)
        return (new_state, jnp.transpose(read, (1, 0, 2)))
    start_state = jnp.zeros((heads, key_width, value_width), jnp.float32)
    _, reads = lax.scan(step, start_state, items)
    outs = reads.reshape(length, heads, value_width)
    return outs * lax.rsqrt(lax.optimization_barrier(jnp.mean(outs * outs, axis=-1, keepdims=True)) + 1e-05) * onorm_gain[None] * jax.nn.silu(gate_out)

def swish_gate(gate, up):
    return jax.nn.silu(gate) * up

def reference(tokens, seg_starts, norm1_gain, w_mix, w_gates, conv_w, decay_rate, onorm_gain, w_out, norm2_gain, w_gu, w_down, cotangent):
    f32 = jnp.float32
    bf16 = jnp.bfloat16
    seqs = seg_starts.shape[0]
    length = tokens.shape[0] // seqs
    mix2d = w_mix.reshape(D, H * MIX)
    gates2d = w_gates.reshape(D, H * 2)
    out2d = w_out.reshape(H * DV, D)
    gu2d = w_gu.reshape(D, 2 * FF)

    def per_sequence(acc, item):
        rows, cot, starts_row = item
        resid = rows.astype(f32)
        normed1 = rms_norm(resid, norm1_gain).astype(bf16)
        proj = jnp.dot(normed1, mix2d, preferred_element_type=f32).reshape(length, H, MIX)
        gates_pre = jnp.dot(normed1, gates2d, preferred_element_type=f32).reshape(length, H, 2)
        seg, before = segment_ids(starts_row, length)

        def mixer(p, g, c, r, o):
            return core(p, g, c, r, o, seg, before)
        heads_out, mixer_back = jax.vjp(mixer, proj, gates_pre, conv_w, decay_rate, onorm_gain)
        mixed = heads_out.astype(bf16).reshape(length, H * DV)
        resid2 = resid + jnp.dot(mixed, out2d, preferred_element_type=f32)
        normed2 = rms_norm(resid2, norm2_gain).astype(bf16)
        gu = jnp.dot(normed2, gu2d, preferred_element_type=f32).reshape(length, 2, FF)
        act = swish_gate(gu[:, 0], gu[:, 1]).astype(bf16)
        output = (resid2 + jnp.dot(act, w_down, preferred_element_type=f32)).astype(bf16)
        g_down = jnp.dot(act.T, cot, preferred_element_type=f32)
        d_act = jnp.dot(cot, w_down.T, preferred_element_type=f32)
        _, swish_back = jax.vjp(swish_gate, gu[:, 0], gu[:, 1])
        d_gate, d_up = swish_back(d_act)
        d_gu = jnp.stack([d_gate, d_up], axis=1).astype(bf16).reshape(length, 2 * FF)
        g_gu = jnp.dot(normed2.T, d_gu, preferred_element_type=f32)
        d_normed2 = jnp.dot(d_gu, gu2d.T, preferred_element_type=f32)
        _, norm2_back = jax.vjp(rms_norm, resid2, norm2_gain)
        d_resid_ffn, g_gain2 = norm2_back(d_normed2)
        d_resid2 = cot.astype(f32) + d_resid_ffn
        d_rows = d_resid2.astype(bf16)
        g_out = jnp.dot(mixed.T, d_rows, preferred_element_type=f32)
        d_heads = jnp.dot(d_rows, out2d.T, preferred_element_type=f32).reshape(length, H, DV)
        d_proj, d_gates_pre, g_conv, g_rate, g_onorm = mixer_back(d_heads)
        d_proj_b = d_proj.astype(bf16).reshape(length, H * MIX)
        d_gates_b = d_gates_pre.astype(bf16).reshape(length, H * 2)
        g_mix = jnp.dot(normed1.T, d_proj_b, preferred_element_type=f32)
        g_gates = jnp.dot(normed1.T, d_gates_b, preferred_element_type=f32)
        d_normed1 = jnp.dot(d_proj_b, mix2d.T, preferred_element_type=f32) + jnp.dot(d_gates_b, gates2d.T, preferred_element_type=f32)
        _, norm1_back = jax.vjp(rms_norm, resid, norm1_gain)
        d_resid1, g_gain1 = norm1_back(d_normed1)
        grad_rows = (d_resid2 + d_resid1).astype(bf16)
        terms = (g_gain1, g_mix, g_gates, g_conv, g_rate, g_onorm, g_out, g_gain2, g_gu, g_down)
        acc = tuple((a + b for a, b in zip(acc, terms)))
        return (acc, (output, grad_rows))
    zero = (jnp.zeros((D,), f32), jnp.zeros((D, H * MIX), f32), jnp.zeros((D, H * 2), f32), jnp.zeros((4, H, CONV), f32), jnp.zeros((H,), f32), jnp.zeros((H, DV), f32), jnp.zeros((H * DV, D), f32), jnp.zeros((D,), f32), jnp.zeros((D, 2 * FF), f32), jnp.zeros((FF, D), f32))
    items = (tokens.reshape(seqs, length, D), cotangent.reshape(seqs, length, D), seg_starts)
    sums, (outputs, grads) = lax.scan(per_sequence, zero, items)
    g_gain1, g_mix, g_gates, g_conv, g_rate, g_onorm, g_out, g_gain2, g_gu, g_down = sums
    return (outputs.reshape(seqs * length, D), grads.reshape(seqs * length, D), g_gain1, g_mix.reshape(D, H, MIX), g_gates.reshape(D, H, 2), g_conv, g_rate, g_onorm, g_out.reshape(H, DV, D), g_gain2, g_gu.reshape(D, 2, FF), g_down)
```

```python
import functools

import jax
import jax.numpy as jnp
from jax import lax
from jax.experimental import pallas as pl
from jax.experimental.pallas import tpu as pltpu
from jax.sharding import PartitionSpec as P

BLOCK = 64
HALO = 8
HI = lax.Precision.HIGHEST


def contract(a, b, dims, exact=False):
    if exact:
        return lax.dot_general(a, b, (dims, ((), ())), precision=HI, preferred_element_type=jnp.float32)
    a, b = a.astype(jnp.bfloat16), b.astype(jnp.bfloat16)
    return lax.dot_general(a, b, (dims, ((), ())), preferred_element_type=jnp.float32)


NN, NT, TN = ((1,), (0,)), ((1,), (1,)), ((0,), (0,))


@functools.partial(jax.custom_vjp, nondiff_argnums=(2,))
def mm_nn(a, b, exact=False):
    return contract(a, b, NN, exact)


mm_nn.defvjp(
    lambda a, b, exact: (contract(a, b, NN, exact), (a, b)),
    lambda exact, res, g: (contract(g, res[1], NT, exact), contract(res[0], g, TN, exact)),
)


@functools.partial(jax.custom_vjp, nondiff_argnums=(2,))
def mm_nt(a, b, exact=False):
    return contract(a, b, NT, exact)


mm_nt.defvjp(
    lambda a, b, exact: (contract(a, b, NT, exact), (a, b)),
    lambda exact, res, g: (contract(g, res[1], NN, exact), contract(g, res[0], TN, exact)),
)


@functools.partial(jax.custom_vjp, nondiff_argnums=(2,))
def mm_tn(a, b, exact=False):
    return contract(a, b, TN, exact)


mm_tn.defvjp(
    lambda a, b, exact: (contract(a, b, TN, exact), (a, b)),
    lambda exact, res, g: (contract(res[1], g, NT, exact), contract(res[0], g, NN, exact)),
)


@jax.custom_vjp
def solve(lower, rhs, inverse):
    return contract(inverse, rhs, NN)


def solve_fwd(lower, rhs, inverse):
    errs = contract(inverse, rhs, NN)
    return errs, (inverse, errs)


def solve_bwd(res, g):
    inverse, errs = res
    d_rhs = contract(inverse, g, TN)
    return -contract(d_rhs, errs, NT), d_rhs, jnp.zeros_like(inverse)


solve.defvjp(solve_fwd, solve_bwd)


@functools.partial(jax.custom_vjp, nondiff_argnums=(1,))
def keepsum(x, axis):
    return jnp.sum(x, axis=axis, keepdims=True)


keepsum.defvjp(
    lambda x, axis: (jnp.sum(x, axis=axis, keepdims=True), x),
    lambda axis, x, g: (jnp.broadcast_to(g, x.shape),),
)


@functools.partial(jax.custom_vjp, nondiff_argnums=(1,))
def spread(x, shape):
    return jnp.broadcast_to(x, shape)


def spread_bwd(shape, x, g):
    for axis in range(2):
        if x.shape[axis] == 1 and shape[axis] != 1:
            g = jnp.sum(g, axis=axis, keepdims=True)
    return (g,)


spread.defvjp(lambda x, shape: (jnp.broadcast_to(x, shape), x), spread_bwd)


@functools.partial(jax.custom_vjp, nondiff_argnums=(1,))
def lagged(ext, lag):
    return pltpu.roll(ext, lag, 0)[HALO:] if lag else ext[HALO:]


def lagged_bwd(lag, ext, g):
    full = jnp.concatenate([jnp.zeros((HALO, g.shape[1]), g.dtype), g], axis=0)
    return (pltpu.roll(full, full.shape[0] - lag, 0) if lag else full,)


lagged.defvjp(lambda ext, lag: (lagged(ext, lag), ext), lagged_bwd)


@jax.custom_vjp
def softplus(x):
    return jnp.maximum(x, 0.0) + jnp.log1p(jnp.exp(-jnp.abs(x)))


softplus.defvjp(lambda x: (softplus(x), x), lambda x, g: (g * jax.nn.sigmoid(x),))


def silu(x):
    return x * jax.nn.sigmoid(x)


def rms_norm(rows, gain):
    return rows * lax.rsqrt(jnp.mean(rows * rows, axis=-1, keepdims=True) + 1e-06) * gain


def segment_ids(starts_row, length):
    places = jnp.arange(length, dtype=jnp.int32)
    flags = jnp.any(starts_row[:, None] == places[None, :], axis=0).astype(jnp.int32)
    seg = jnp.cumsum(flags)
    before = jnp.concatenate([seg[:1], seg[:-1]])
    columns = [seg]
    for lag in range(1, 4):
        moved = jnp.pad(seg, (lag, 0), constant_values=-1)[:length]
        columns.append(moved == seg)
    columns.append(seg == jnp.repeat(before[::BLOCK], BLOCK))
    columns += [jnp.zeros_like(seg)] * 3
    return jnp.stack([c.astype(jnp.float32) for c in columns], axis=1)


def masks():
    shape = (BLOCK, BLOCK)
    row = lax.broadcasted_iota(jnp.int32, shape, 0)
    col = lax.broadcasted_iota(jnp.int32, shape, 1)
    return row, col


def unit_inverse(lowers):
    row, col = masks()
    out = None
    size = 0
    while (1 << size) < BLOCK:
        part = jnp.logical_and(
            (row >> (size + 1)) == (col >> (size + 1)),
            jnp.logical_and(((row >> size) & 1) == 1, ((col >> size) & 1) == 0),
        )
        cut = [jnp.where(part, low, 0.0) for low in lowers]
        if out is None:
            unit = (row == col).astype(jnp.float32)
            out = [unit - c for c in cut]
        else:
            mid = [contract(c, t, NN, True) for c, t in zip(cut, out)]
            out = [t - contract(t, m, NN, True) for t, m in zip(out, mid)]
        size += 1
    return out


def front(ext, alpha_pre, beta_pre, taps, rate, aux, key_width):
    rows = BLOCK
    wide = (rows, ext.shape[1])
    square = (BLOCK, BLOCK)
    total = spread(taps[3], wide) * lagged(ext, 0)
    for lag in range(1, 4):
        keep = jnp.broadcast_to(aux[lag], wide)
        total = total + spread(taps[3 - lag], wide) * (lagged(ext, lag) * keep)
    act = silu(total)

    def unit_rows(x):
        return x * spread(lax.rsqrt(keepsum(x * x, 1) + 1e-06), x.shape)

    return act, unit_rows


def block_terms(query, keys, beta_pre, alpha_pre, rate, aux):
    square = (BLOCK, BLOCK)
    row, col = masks()
    eye = (row == col).astype(jnp.float32)
    seg_col = jnp.broadcast_to(aux[0], square)
    seg_row = jnp.broadcast_to(jnp.sum(eye * seg_col, axis=0, keepdims=True), square)
    live = jnp.logical_and(seg_col == seg_row, row >= col)
    beta = jax.nn.sigmoid(beta_pre)
    logd = -spread(rate, alpha_pre.shape) * softplus(alpha_pre)
    incl = (row >= col).astype(jnp.float32)
    logd_row = keepsum(eye * spread(logd, square), 0)
    cum = keepsum(incl * spread(logd_row, square), 1)
    cum_row = keepsum(eye * spread(cum, square), 0)
    diff = spread(cum, square) - spread(cum_row, square)
    within = jnp.where(live, jnp.exp(jnp.where(live, diff, 0.0)), 0.0)
    carried = jnp.exp(cum) * aux[4]
    kk = mm_nt(keys, keys, True)
    strict = (row > col).astype(jnp.float32)
    lower = spread(beta, square) * within * kk * strict
    place = lax.broadcasted_iota(jnp.int32, (BLOCK, 1), 0)
    last = (place == BLOCK - 1).astype(jnp.float32)
    cum_last = spread(keepsum(cum * last, 0), cum.shape)
    seg_last = jnp.broadcast_to(jnp.sum(aux[0] * last, axis=0, keepdims=True), cum.shape)
    same = seg_last == aux[0]
    final = jnp.where(same, jnp.exp(jnp.where(same, cum_last - cum, 0.0)), 0.0)
    carried_last = keepsum(carried * last, 0)
    return beta, within, carried, lower, final, carried_last


def split_heads(ext, taps, aux, key_width):
    act, unit_rows = front(ext, None, None, taps, None, aux, key_width)
    query = unit_rows(act[:, :key_width]) * key_width ** (-0.5)
    keys = unit_rows(act[:, key_width : 2 * key_width])
    return query, keys, act[:, 2 * key_width :]


def advance(query, keys, values, terms, state, inverse, gate_out, onorm):
    beta, within, carried, lower, final, carried_last = terms
    tall = values.shape
    rhs = spread(beta, tall) * (values - spread(carried, tall) * mm_nn(keys, state))
    errs = solve(lower, rhs, inverse)
    read = spread(carried, tall) * mm_nn(query, state)
    read = read + mm_nn(within * mm_nt(query, keys), errs)
    new_state = spread(carried_last, state.shape) * state
    new_state = new_state + mm_tn(spread(final, keys.shape) * keys, errs)
    scale = lax.rsqrt(keepsum(read * read, 1) * (1.0 / tall[1]) + 1e-05)
    out = read * spread(scale, tall) * spread(onorm, tall) * silu(gate_out)
    return out, new_state


def head_inputs(h, dims, halo_ref, proj_ref, gates_ref, conv_ref, rate_ref, onorm_ref):
    heads, mix, conv, value = dims
    base = h * mix
    ext = jnp.concatenate(
        [halo_ref[:, base : base + conv], proj_ref[:, base : base + conv]], axis=0
    )
    gate_out = proj_ref[:, base + conv : base + mix]
    alpha_pre = gates_ref[:, 2 * h : 2 * h + 1]
    beta_pre = gates_ref[:, 2 * h + 1 : 2 * h + 2]
    taps = tuple(conv_ref[i : i + 1, h * conv : (h + 1) * conv] for i in range(4))
    rate = rate_ref[:, h : h + 1]
    onorm = onorm_ref[h : h + 1, :]
    return ext, gate_out, alpha_pre, beta_pre, taps, rate, onorm


def forward_kernel(dims, halo_ref, proj_ref, gates_ref, aux_ref, conv_ref, rate_ref, onorm_ref,
                   out_ref, states_ref, inv_ref, state):
    heads, mix, conv, value = dims
    key_width = (conv - value) // 2

    @pl.when(pl.program_id(1) == 0)
    def _():
        state[...] = jnp.zeros_like(state)

    aux = [aux_ref[:, i : i + 1] for i in range(5)]
    work = []
    for h in range(heads):
        ext, gate_out, alpha_pre, beta_pre, taps, rate, onorm = head_inputs(
            h, dims, halo_ref, proj_ref, gates_ref, conv_ref, rate_ref, onorm_ref
        )
        query, keys, values = split_heads(ext, taps, aux, key_width)
        terms = block_terms(query, keys, beta_pre, alpha_pre, rate, aux)
        work.append((query, keys, values, terms, gate_out, onorm))
    inverses = unit_inverse([w[3][3] for w in work])
    for h in range(heads):
        query, keys, values, terms, gate_out, onorm = work[h]
        old = state[h * key_width : (h + 1) * key_width, :]
        out, new = advance(query, keys, values, terms, old, inverses[h], gate_out, onorm)
        states_ref[0, h * key_width : (h + 1) * key_width, :] = old
        state[h * key_width : (h + 1) * key_width, :] = new
        inv_ref[0, h * BLOCK : (h + 1) * BLOCK, :] = inverses[h]
        out_ref[:, h * value : (h + 1) * value] = out.astype(out_ref.dtype)


def backward_kernel(dims, halo_ref, proj_ref, gates_ref, aux_ref, conv_ref, rate_ref, onorm_ref,
                    states_ref, inv_ref, d_out_ref,
                    d_proj_ref, d_gates_ref, d_conv_ref, d_rate_ref, d_onorm_ref, d_state, spill):
    heads, mix, conv, value = dims
    key_width = (conv - value) // 2

    @pl.when(pl.program_id(1) == 0)
    def _():
        d_state[...] = jnp.zeros_like(d_state)
        spill[...] = jnp.zeros_like(spill)

    @pl.when(jnp.logical_and(pl.program_id(0) == 0, pl.program_id(1) == 0))
    def _():
        d_conv_ref[...] = jnp.zeros_like(d_conv_ref)
        d_rate_ref[...] = jnp.zeros_like(d_rate_ref)
        d_onorm_ref[...] = jnp.zeros_like(d_onorm_ref)

    aux = [aux_ref[:, i : i + 1] for i in range(5)]
    lane = lax.broadcasted_iota(jnp.int32, (BLOCK, 2 * heads), 1)
    d_gates = jnp.zeros((BLOCK, 2 * heads), jnp.float32)
    for h in range(heads):
        ext, gate_out, alpha_pre, beta_pre, taps, rate, onorm = head_inputs(
            h, dims, halo_ref, proj_ref, gates_ref, conv_ref, rate_ref, onorm_ref
        )
        old = states_ref[0, h * key_width : (h + 1) * key_width, :]
        inverse = inv_ref[0, h * BLOCK : (h + 1) * BLOCK, :]

        act, act_back = jax.vjp(
            lambda e, t: front(e, None, None, t, None, aux, key_width)[0], ext, taps
        )
        raw_q = act[:, :key_width]
        raw_k = act[:, key_width : 2 * key_width]
        values = act[:, 2 * key_width :]

        def rest(raw_q, raw_k, values, gate_out, alpha_pre, beta_pre, rate, onorm, old):
            def unit_rows(x):
                return x * spread(lax.rsqrt(keepsum(x * x, 1) + 1e-06), x.shape)

            query = unit_rows(raw_q) * key_width ** (-0.5)
            keys = unit_rows(raw_k)
            terms = block_terms(query, keys, beta_pre, alpha_pre, rate, aux)
            return advance(query, keys, values, terms, old, inverse, gate_out, onorm)

        _, back = jax.vjp(
            rest, raw_q, raw_k, values, gate_out, alpha_pre, beta_pre, rate, onorm, old
        )
        d_out = d_out_ref[:, h * value : (h + 1) * value]
        span = slice(h * key_width, (h + 1) * key_width)
        d_q, d_k, d_v, d_gate, d_alpha, d_beta, d_rate, d_onorm, d_old = back(
            (d_out, d_state[span, :])
        )
        d_state[span, :] = d_old
        d_ext, d_taps = act_back(jnp.concatenate([d_q, d_k, d_v], axis=1))
        cols = slice(h * conv, (h + 1) * conv)
        carry = jnp.concatenate(
            [jnp.zeros((BLOCK - HALO, conv), jnp.float32), spill[:, cols]], axis=0
        )
        d_mixed = d_ext[HALO:] + carry
        spill[:, cols] = d_ext[:HALO]
        base = h * mix
        d_proj_ref[:, base : base + conv] = d_mixed.astype(d_proj_ref.dtype)
        d_proj_ref[:, base + conv : base + mix] = d_gate.astype(d_proj_ref.dtype)
        for i in range(4):
            d_conv_ref[i : i + 1, cols] += d_taps[i]
        d_rate_ref[h : h + 1, :] += jnp.broadcast_to(d_rate, (1, 128))
        d_onorm_ref[h : h + 1, :] += d_onorm
        d_gates = d_gates + jnp.where(lane == 2 * h, jnp.broadcast_to(d_alpha, lane.shape), 0.0)
        d_gates = d_gates + jnp.where(lane == 2 * h + 1, jnp.broadcast_to(d_beta, lane.shape), 0.0)
    d_gates_ref[...] = d_gates.astype(d_gates_ref.dtype)


def common_specs(dims, blocks, order):
    heads, mix, conv, value = dims
    ratio = BLOCK // HALO
    at = lambda s, b: s * blocks + order(b)
    return [
        pl.BlockSpec((HALO, heads * mix), lambda s, b: (jnp.maximum(at(s, b) * ratio - 1, 0), 0)),
        pl.BlockSpec((BLOCK, heads * mix), lambda s, b: (at(s, b), 0)),
        pl.BlockSpec((BLOCK, heads * 2), lambda s, b: (at(s, b), 0)),
        pl.BlockSpec((BLOCK, 8), lambda s, b: (at(s, b), 0)),
        pl.BlockSpec((4, heads * conv), lambda s, b: (0, 0)),
        pl.BlockSpec((1, heads), lambda s, b: (0, 0)),
        pl.BlockSpec((heads, value), lambda s, b: (0, 0)),
    ], at


def mixer_forward(proj, gates_pre, aux, conv2d, rate, onorm, dims, seqs, interpret=False):
    heads, mix, conv, value = dims
    key_width = (conv - value) // 2
    rows = proj.shape[0]
    blocks = rows // seqs // BLOCK
    specs, at = common_specs(dims, blocks, lambda b: b)
    return pl.pallas_call(
        functools.partial(forward_kernel, dims),
        grid=(seqs, blocks),
        in_specs=specs,
        out_specs=[
            pl.BlockSpec((BLOCK, heads * value), lambda s, b: (at(s, b), 0)),
            pl.BlockSpec((1, heads * key_width, value), lambda s, b: (at(s, b), 0, 0)),
            pl.BlockSpec((1, heads * BLOCK, BLOCK), lambda s, b: (at(s, b), 0, 0)),
        ],
        out_shape=[
            jax.ShapeDtypeStruct((rows, heads * value), jnp.bfloat16),
            jax.ShapeDtypeStruct((seqs * blocks, heads * key_width, value), jnp.float32),
            jax.ShapeDtypeStruct((seqs * blocks, heads * BLOCK, BLOCK), jnp.float32),
        ],
        scratch_shapes=[pltpu.VMEM((heads * key_width, value), jnp.float32)],
        cost_estimate=pl.CostEstimate(flops=rows * heads * 2000000, bytes_accessed=rows * heads * 8192, transcendentals=0),
        name="mixer_forward",
        interpret=interpret,
    )(proj, proj, gates_pre, aux, conv2d, rate, onorm)


def mixer_backward(proj, gates_pre, aux, conv2d, rate, onorm, states, inverses, d_heads, dims, seqs, interpret=False):
    heads, mix, conv, value = dims
    key_width = (conv - value) // 2
    rows = proj.shape[0]
    blocks = rows // seqs // BLOCK
    specs, at = common_specs(dims, blocks, lambda b: blocks - 1 - b)
    return pl.pallas_call(
        functools.partial(backward_kernel, dims),
        grid=(seqs, blocks),
        in_specs=specs + [
            pl.BlockSpec((1, heads * key_width, value), lambda s, b: (at(s, b), 0, 0)),
            pl.BlockSpec((1, heads * BLOCK, BLOCK), lambda s, b: (at(s, b), 0, 0)),
            pl.BlockSpec((BLOCK, heads * value), lambda s, b: (at(s, b), 0)),
        ],
        out_specs=[
            pl.BlockSpec((BLOCK, heads * mix), lambda s, b: (at(s, b), 0)),
            pl.BlockSpec((BLOCK, heads * 2), lambda s, b: (at(s, b), 0)),
            pl.BlockSpec((4, heads * conv), lambda s, b: (0, 0)),
            pl.BlockSpec((heads, 128), lambda s, b: (0, 0)),
            pl.BlockSpec((heads, value), lambda s, b: (0, 0)),
        ],
        out_shape=[
            jax.ShapeDtypeStruct((rows, heads * mix), jnp.bfloat16),
            jax.ShapeDtypeStruct((rows, heads * 2), jnp.bfloat16),
            jax.ShapeDtypeStruct((4, heads * conv), jnp.float32),
            jax.ShapeDtypeStruct((heads, 128), jnp.float32),
            jax.ShapeDtypeStruct((heads, value), jnp.float32),
        ],
        scratch_shapes=[
            pltpu.VMEM((heads * key_width, value), jnp.float32),
            pltpu.VMEM((HALO, heads * conv), jnp.float32),
        ],
        cost_estimate=pl.CostEstimate(flops=rows * heads * 5000000, bytes_accessed=rows * heads * 12288, transcendentals=0),
        name="mixer_backward",
        interpret=interpret,
    )(proj, proj, gates_pre, aux, conv2d, rate, onorm, states, inverses, d_heads)


def swish_gate(gate, up):
    return jax.nn.silu(gate) * up


def local(
    tokens,
    seg_starts,
    norm1_gain,
    w_mix,
    w_gates,
    conv_w,
    decay_rate,
    onorm_gain,
    w_out,
    norm2_gain,
    w_gu,
    w_down,
    cotangent,
):
    f32 = jnp.float32
    bf16 = jnp.bfloat16
    local_rows, width = tokens.shape
    seqs = seg_starts.shape[0]
    heads = w_mix.shape[1]
    mix_cols = w_mix.shape[2]
    value_width = onorm_gain.shape[1]
    hidden = w_down.shape[0]
    mix2d = w_mix.reshape(width, heads * mix_cols)
    gates2d = w_gates.reshape(width, heads * 2)
    out2d = w_out.reshape(heads * value_width, width)
    gu2d = w_gu.reshape(width, 2 * hidden)
    resid = tokens.astype(f32)
    normed1 = rms_norm(resid, norm1_gain).astype(bf16)
    rows1 = lax.all_gather(normed1, "tensor", axis=0, tiled=True)
    total_rows = rows1.shape[0]
    length = total_rows // seqs
    dims = (heads, mix_cols, conv_w.shape[2], value_width)
    proj = jnp.dot(rows1, mix2d, preferred_element_type=f32)
    gates_pre = jnp.dot(rows1, gates2d, preferred_element_type=f32)
    aux = jax.vmap(segment_ids, in_axes=(0, None))(seg_starts, length).reshape(total_rows, 8)
    mixer_args = (proj, gates_pre, aux, conv_w.reshape(4, -1), decay_rate[None, :], onorm_gain)
    mixed, states, inverses = mixer_forward(*mixer_args, dims, seqs)
    resid2 = resid + lax.psum_scatter(
        jnp.dot(mixed, out2d, preferred_element_type=f32).astype(jnp.bfloat16),
        "tensor",
        scatter_dimension=0,
        tiled=True,
    ).astype(jnp.float32)
    normed2 = rms_norm(resid2, norm2_gain).astype(bf16)
    rows2 = lax.all_gather(normed2, "tensor", axis=0, tiled=True)
    gu = jnp.dot(rows2, gu2d, preferred_element_type=f32).reshape(total_rows, 2, hidden)
    act = swish_gate(gu[:, 0], gu[:, 1]).astype(bf16)
    output = (
        resid2
        + lax.psum_scatter(
            jnp.dot(act, w_down, preferred_element_type=f32).astype(jnp.bfloat16),
            "tensor",
            scatter_dimension=0,
            tiled=True,
        ).astype(jnp.float32)
    ).astype(bf16)
    cot_rows = lax.all_gather(cotangent, "tensor", axis=0, tiled=True)
    grad_down = jnp.dot(act.T, cot_rows, preferred_element_type=f32)
    d_act = jnp.dot(cot_rows, w_down.T, preferred_element_type=f32)
    _, swish_back = jax.vjp(swish_gate, gu[:, 0], gu[:, 1])
    d_gate, d_up = swish_back(d_act)
    d_gu = jnp.stack([d_gate, d_up], axis=1).astype(bf16).reshape(total_rows, 2 * hidden)
    grad_gu = jnp.dot(rows2.T, d_gu, preferred_element_type=f32).reshape(width, 2, hidden)
    d_normed2 = lax.psum_scatter(
        jnp.dot(d_gu, gu2d.T, preferred_element_type=f32).astype(jnp.bfloat16),
        "tensor",
        scatter_dimension=0,
        tiled=True,
    ).astype(jnp.float32)
    _, norm2_back = jax.vjp(rms_norm, resid2, norm2_gain)
    d_resid_ffn, gain2_part = norm2_back(d_normed2)
    d_resid2 = cotangent.astype(f32) + d_resid_ffn
    d_rows = lax.all_gather(d_resid2.astype(bf16), "tensor", axis=0, tiled=True)
    grad_out = jnp.dot(mixed.T, d_rows, preferred_element_type=f32).reshape(
        heads, value_width, width
    )
    d_heads = jnp.dot(d_rows, out2d.T, preferred_element_type=f32)
    d_proj_b, d_gates_b, d_conv, d_rate, d_onorm = mixer_backward(
        *mixer_args, states, inverses, d_heads, dims, seqs
    )
    d_conv = d_conv.reshape(conv_w.shape)
    d_rate = d_rate[:, 0]
    grad_mix = jnp.dot(rows1.T, d_proj_b, preferred_element_type=f32)
    grad_gates = jnp.dot(rows1.T, d_gates_b, preferred_element_type=f32).reshape(width, heads, 2)
    d_normed1 = lax.psum_scatter(
        (
            jnp.dot(d_proj_b, mix2d.T, preferred_element_type=f32)
            + jnp.dot(d_gates_b, gates2d.T, preferred_element_type=f32)
        ).astype(jnp.bfloat16),
        "tensor",
        scatter_dimension=0,
        tiled=True,
    ).astype(jnp.float32)
    _, norm1_back = jax.vjp(rms_norm, resid, norm1_gain)
    d_resid1, gain1_part = norm1_back(d_normed1)
    grad_tokens = (d_resid2 + d_resid1).astype(bf16)
    grad_conv, grad_rate, grad_onorm = lax.psum((d_conv, d_rate, d_onorm), "dp")
    mix_share, gates_share, out_share, gu_share, down_share, gain1_share, gain2_share = (
        lax.psum_scatter(grad_mix.astype(bf16), "dp", scatter_dimension=0, tiled=True),
        lax.psum_scatter(grad_gates, "dp", scatter_dimension=0, tiled=True),
        lax.psum_scatter(grad_out.astype(bf16), "dp", scatter_dimension=2, tiled=True),
        lax.psum_scatter(grad_gu.astype(bf16), "dp", scatter_dimension=0, tiled=True),
        lax.psum_scatter(grad_down.astype(bf16), "dp", scatter_dimension=1, tiled=True),
        lax.psum_scatter(gain1_part, "dp", scatter_dimension=0, tiled=True),
        lax.psum_scatter(gain2_part, "dp", scatter_dimension=0, tiled=True),
    )
    mix_share = mix_share.reshape(-1, heads, mix_cols)
    mix_share, out_share, gu_share, down_share = (
        share.astype(f32) for share in (mix_share, out_share, gu_share, down_share)
    )
    gain1_total, gain2_total = lax.psum((gain1_share, gain2_share), "tensor")
    return (
        output,
        grad_tokens,
        gain1_total,
        mix_share,
        gates_share,
        grad_conv,
        grad_rate,
        grad_onorm,
        out_share,
        gain2_total,
        gu_share,
        down_share,
    )


def solution(mesh):
    in_specs = (
        P(("dp", "tensor"), None),
        P("dp", None),
        P(),
        P(None, "tensor", None),
        P(None, "tensor", None),
        P(None, "tensor", None),
        P("tensor"),
        P("tensor", None),
        P("tensor", None, None),
        P(),
        P(None, None, "tensor"),
        P("tensor", None),
        P(("dp", "tensor"), None),
    )
    out_specs = (
        P(("dp", "tensor"), None),
        P(("dp", "tensor"), None),
        P("dp"),
        P("dp", "tensor", None),
        P("dp", "tensor", None),
        P(None, "tensor", None),
        P("tensor"),
        P("tensor", None),
        P("tensor", None, "dp"),
        P("dp"),
        P("dp", None, "tensor"),
        P("tensor", "dp"),
    )
    return jax.shard_map(local, mesh=mesh, in_specs=in_specs, out_specs=out_specs, check_vma=False)
```

```python
import functools

import jax
import jax.numpy as jnp
from jax import lax
from jax.experimental import pallas as pl
from jax.experimental.pallas import tpu as pltpu
from jax.sharding import PartitionSpec as P

BLOCK = 64
HALO = 8
HI = lax.Precision.HIGHEST


def contract(a, b, dims, exact=False):
    if exact:
        return lax.dot_general(a, b, (dims, ((), ())), precision=HI, preferred_element_type=jnp.float32)
    a, b = a.astype(jnp.bfloat16), b.astype(jnp.bfloat16)
    return lax.dot_general(a, b, (dims, ((), ())), preferred_element_type=jnp.float32)


NN, NT, TN = ((1,), (0,)), ((1,), (1,)), ((0,), (0,))


@functools.partial(jax.custom_vjp, nondiff_argnums=(2,))
def mm_nn(a, b, exact=False):
    return contract(a, b, NN, exact)


mm_nn.defvjp(
    lambda a, b, exact: (contract(a, b, NN, exact), (a, b)),
    lambda exact, res, g: (contract(g, res[1], NT, exact), contract(res[0], g, TN, exact)),
)


@functools.partial(jax.custom_vjp, nondiff_argnums=(2,))
def mm_nt(a, b, exact=False):
    return contract(a, b, NT, exact)


mm_nt.defvjp(
    lambda a, b, exact: (contract(a, b, NT, exact), (a, b)),
    lambda exact, res, g: (contract(g, res[1], NN, exact), contract(g, res[0], TN, exact)),
)


@functools.partial(jax.custom_vjp, nondiff_argnums=(2,))
def mm_tn(a, b, exact=False):
    return contract(a, b, TN, exact)


mm_tn.defvjp(
    lambda a, b, exact: (contract(a, b, TN, exact), (a, b)),
    lambda exact, res, g: (contract(res[1], g, NT, exact), contract(res[0], g, NN, exact)),
)


@jax.custom_vjp
def solve(lower, rhs, inverse):
    return contract(inverse, rhs, NN)


def solve_fwd(lower, rhs, inverse):
    errs = contract(inverse, rhs, NN)
    return errs, (inverse, errs)


def solve_bwd(res, g):
    inverse, errs = res
    d_rhs = contract(inverse, g, TN)
    return -contract(d_rhs, errs, NT), d_rhs, jnp.zeros_like(inverse)


solve.defvjp(solve_fwd, solve_bwd)


@functools.partial(jax.custom_vjp, nondiff_argnums=(1,))
def keepsum(x, axis):
    return jnp.sum(x, axis=axis, keepdims=True)


keepsum.defvjp(
    lambda x, axis: (jnp.sum(x, axis=axis, keepdims=True), x),
    lambda axis, x, g: (jnp.broadcast_to(g, x.shape),),
)


@functools.partial(jax.custom_vjp, nondiff_argnums=(1,))
def spread(x, shape):
    return jnp.broadcast_to(x, shape)


def spread_bwd(shape, x, g):
    for axis in range(2):
        if x.shape[axis] == 1 and shape[axis] != 1:
            g = jnp.sum(g, axis=axis, keepdims=True)
    return (g,)


spread.defvjp(lambda x, shape: (jnp.broadcast_to(x, shape), x), spread_bwd)


@functools.partial(jax.custom_vjp, nondiff_argnums=(1,))
def lagged(ext, lag):
    return pltpu.roll(ext, lag, 0)[HALO:] if lag else ext[HALO:]


def lagged_bwd(lag, ext, g):
    full = jnp.concatenate([jnp.zeros((HALO, g.shape[1]), g.dtype), g], axis=0)
    return (pltpu.roll(full, full.shape[0] - lag, 0) if lag else full,)


lagged.defvjp(lambda ext, lag: (lagged(ext, lag), ext), lagged_bwd)


@jax.custom_vjp
def softplus(x):
    return jnp.maximum(x, 0.0) + jnp.log1p(jnp.exp(-jnp.abs(x)))


softplus.defvjp(lambda x: (softplus(x), x), lambda x, g: (g * jax.nn.sigmoid(x),))


def silu(x):
    return x * jax.nn.sigmoid(x)


def rms_norm(rows, gain):
    return rows * lax.rsqrt(jnp.mean(rows * rows, axis=-1, keepdims=True) + 1e-06) * gain


def segment_ids(starts_row, length):
    places = jnp.arange(length, dtype=jnp.int32)
    flags = jnp.any(starts_row[:, None] == places[None, :], axis=0).astype(jnp.int32)
    seg = jnp.cumsum(flags)
    before = jnp.concatenate([seg[:1], seg[:-1]])
    columns = [seg]
    for lag in range(1, 4):
        moved = jnp.pad(seg, (lag, 0), constant_values=-1)[:length]
        columns.append(moved == seg)
    columns.append(seg == jnp.repeat(before[::BLOCK], BLOCK))
    columns += [jnp.zeros_like(seg)] * 3
    return jnp.stack([c.astype(jnp.float32) for c in columns], axis=1)


def masks():
    shape = (BLOCK, BLOCK)
    row = lax.broadcasted_iota(jnp.int32, shape, 0)
    col = lax.broadcasted_iota(jnp.int32, shape, 1)
    return row, col


def unit_inverse(lowers):
    row, col = masks()
    out = None
    size = 0
    while (1 << size) < BLOCK:
        part = jnp.logical_and(
            (row >> (size + 1)) == (col >> (size + 1)),
            jnp.logical_and(((row >> size) & 1) == 1, ((col >> size) & 1) == 0),
        )
        cut = [jnp.where(part, low, 0.0) for low in lowers]
        if out is None:
            unit = (row == col).astype(jnp.float32)
            out = [unit - c for c in cut]
        else:
            mid = [contract(c, t, NN, True) for c, t in zip(cut, out)]
            out = [t - contract(t, m, NN, True) for t, m in zip(out, mid)]
        size += 1
    return out


def front(ext, alpha_pre, beta_pre, taps, rate, aux, key_width):
    rows = BLOCK
    wide = (rows, ext.shape[1])
    square = (BLOCK, BLOCK)
    total = spread(taps[3], wide) * lagged(ext, 0)
    for lag in range(1, 4):
        keep = jnp.broadcast_to(aux[lag], wide)
        total = total + spread(taps[3 - lag], wide) * (lagged(ext, lag) * keep)
    act = silu(total)

    def unit_rows(x):
        return x * spread(lax.rsqrt(keepsum(x * x, 1) + 1e-06), x.shape)

    return act, unit_rows


def block_terms(query, keys, beta_pre, alpha_pre, rate, aux):
    square = (BLOCK, BLOCK)
    row, col = masks()
    eye = (row == col).astype(jnp.float32)
    seg_col = jnp.broadcast_to(aux[0], square)
    seg_row = jnp.broadcast_to(jnp.sum(eye * seg_col, axis=0, keepdims=True), square)
    live = jnp.logical_and(seg_col == seg_row, row >= col)
    beta = jax.nn.sigmoid(beta_pre)
    logd = -spread(rate, alpha_pre.shape) * softplus(alpha_pre)
    incl = (row >= col).astype(jnp.float32)
    logd_row = keepsum(eye * spread(logd, square), 0)
    cum = keepsum(incl * spread(logd_row, square), 1)
    cum_row = keepsum(eye * spread(cum, square), 0)
    diff = spread(cum, square) - spread(cum_row, square)
    within = jnp.where(live, jnp.exp(jnp.where(live, diff, 0.0)), 0.0)
    carried = jnp.exp(cum) * aux[4]
    kk = mm_nt(keys, keys, True)
    strict = (row > col).astype(jnp.float32)
    lower = spread(beta, square) * within * kk * strict
    place = lax.broadcasted_iota(jnp.int32, (BLOCK, 1), 0)
    last = (place == BLOCK - 1).astype(jnp.float32)
    cum_last = spread(keepsum(cum * last, 0), cum.shape)
    seg_last = jnp.broadcast_to(jnp.sum(aux[0] * last, axis=0, keepdims=True), cum.shape)
    same = seg_last == aux[0]
    final = jnp.where(same, jnp.exp(jnp.where(same, cum_last - cum, 0.0)), 0.0)
    carried_last = keepsum(carried * last, 0)
    return beta, within, carried, lower, final, carried_last


def split_heads(ext, taps, aux, key_width):
    act, unit_rows = front(ext, None, None, taps, None, aux, key_width)
    query = unit_rows(act[:, :key_width]) * key_width ** (-0.5)
    keys = unit_rows(act[:, key_width : 2 * key_width])
    return query, keys, act[:, 2 * key_width :]


def advance(query, keys, values, terms, state, inverse, gate_out, onorm):
    beta, within, carried, lower, final, carried_last = terms
    tall = values.shape
    rhs = spread(beta, tall) * (values - spread(carried, tall) * mm_nn(keys, state))
    errs = solve(lower, rhs, inverse)
    read = spread(carried, tall) * mm_nn(query, state)
    read = read + mm_nn(within * mm_nt(query, keys), errs)
    new_state = spread(carried_last, state.shape) * state
    new_state = new_state + mm_tn(spread(final, keys.shape) * keys, errs)
    scale = lax.rsqrt(keepsum(read * read, 1) * (1.0 / tall[1]) + 1e-05)
    out = read * spread(scale, tall) * spread(onorm, tall) * silu(gate_out)
    return out, new_state


def head_inputs(h, dims, halo_ref, proj_ref, gates_ref, conv_ref, rate_ref, onorm_ref):
    heads, mix, conv, value = dims
    base = h * mix
    ext = jnp.concatenate(
        [halo_ref[:, base : base + conv], proj_ref[:, base : base + conv]], axis=0
    )
    gate_out = proj_ref[:, base + conv : base + mix]
    alpha_pre = gates_ref[:, 2 * h : 2 * h + 1]
    beta_pre = gates_ref[:, 2 * h + 1 : 2 * h + 2]
    taps = tuple(conv_ref[i : i + 1, h * conv : (h + 1) * conv] for i in range(4))
    rate = rate_ref[:, h : h + 1]
    onorm = onorm_ref[h : h + 1, :]
    return ext, gate_out, alpha_pre, beta_pre, taps, rate, onorm


def forward_kernel(dims, halo_ref, proj_ref, gates_ref, aux_ref, conv_ref, rate_ref, onorm_ref,
                   out_ref, states_ref, inv_ref, state):
    heads, mix, conv, value = dims
    key_width = (conv - value) // 2

    @pl.when(pl.program_id(1) == 0)
    def _():
        state[...] = jnp.zeros_like(state)

    aux = [aux_ref[:, i : i + 1] for i in range(5)]
    work = []
    for h in range(heads):
        ext, gate_out, alpha_pre, beta_pre, taps, rate, onorm = head_inputs(
            h, dims, halo_ref, proj_ref, gates_ref, conv_ref, rate_ref, onorm_ref
        )
        query, keys, values = split_heads(ext, taps, aux, key_width)
        terms = block_terms(query, keys, beta_pre, alpha_pre, rate, aux)
        work.append((query, keys, values, terms, gate_out, onorm))
    inverses = unit_inverse([w[3][3] for w in work])
    for h in range(heads):
        query, keys, values, terms, gate_out, onorm = work[h]
        old = state[h * key_width : (h + 1) * key_width, :]
        out, new = advance(query, keys, values, terms, old, inverses[h], gate_out, onorm)
        states_ref[0, h * key_width : (h + 1) * key_width, :] = old
        state[h * key_width : (h + 1) * key_width, :] = new
        inv_ref[0, h * BLOCK : (h + 1) * BLOCK, :] = inverses[h]
        out_ref[:, h * value : (h + 1) * value] = out.astype(out_ref.dtype)


def backward_kernel(dims, halo_ref, proj_ref, gates_ref, aux_ref, conv_ref, rate_ref, onorm_ref,
                    states_ref, inv_ref, d_out_ref,
                    d_proj_ref, d_gates_ref, d_conv_ref, d_rate_ref, d_onorm_ref, d_state, spill):
    heads, mix, conv, value = dims
    key_width = (conv - value) // 2

    @pl.when(pl.program_id(1) == 0)
    def _():
        d_state[...] = jnp.zeros_like(d_state)
        spill[...] = jnp.zeros_like(spill)

    @pl.when(jnp.logical_and(pl.program_id(0) == 0, pl.program_id(1) == 0))
    def _():
        d_conv_ref[...] = jnp.zeros_like(d_conv_ref)
        d_rate_ref[...] = jnp.zeros_like(d_rate_ref)
        d_onorm_ref[...] = jnp.zeros_like(d_onorm_ref)

    aux = [aux_ref[:, i : i + 1] for i in range(5)]
    lane = lax.broadcasted_iota(jnp.int32, (BLOCK, 2 * heads), 1)
    d_gates = jnp.zeros((BLOCK, 2 * heads), jnp.float32)
    for h in range(heads):
        ext, gate_out, alpha_pre, beta_pre, taps, rate, onorm = head_inputs(
            h, dims, halo_ref, proj_ref, gates_ref, conv_ref, rate_ref, onorm_ref
        )
        old = states_ref[0, h * key_width : (h + 1) * key_width, :]
        inverse = inv_ref[0, h * BLOCK : (h + 1) * BLOCK, :]

        act, act_back = jax.vjp(
            lambda e, t: front(e, None, None, t, None, aux, key_width)[0], ext, taps
        )
        raw_q = act[:, :key_width]
        raw_k = act[:, key_width : 2 * key_width]
        values = act[:, 2 * key_width :]

        def rest(raw_q, raw_k, values, gate_out, alpha_pre, beta_pre, rate, onorm, old):
            def unit_rows(x):
                return x * spread(lax.rsqrt(keepsum(x * x, 1) + 1e-06), x.shape)

            query = unit_rows(raw_q) * key_width ** (-0.5)
            keys = unit_rows(raw_k)
            terms = block_terms(query, keys, beta_pre, alpha_pre, rate, aux)
            return advance(query, keys, values, terms, old, inverse, gate_out, onorm)

        _, back = jax.vjp(
            rest, raw_q, raw_k, values, gate_out, alpha_pre, beta_pre, rate, onorm, old
        )
        d_out = d_out_ref[:, h * value : (h + 1) * value]
        span = slice(h * key_width, (h + 1) * key_width)
        d_q, d_k, d_v, d_gate, d_alpha, d_beta, d_rate, d_onorm, d_old = back(
            (d_out, d_state[span, :])
        )
        d_state[span, :] = d_old
        d_ext, d_taps = act_back(jnp.concatenate([d_q, d_k, d_v], axis=1))
        cols = slice(h * conv, (h + 1) * conv)
        carry = jnp.concatenate(
            [jnp.zeros((BLOCK - HALO, conv), jnp.float32), spill[:, cols]], axis=0
        )
        d_mixed = d_ext[HALO:] + carry
        spill[:, cols] = d_ext[:HALO]
        base = h * mix
        d_proj_ref[:, base : base + conv] = d_mixed.astype(d_proj_ref.dtype)
        d_proj_ref[:, base + conv : base + mix] = d_gate.astype(d_proj_ref.dtype)
        for i in range(4):
            d_conv_ref[i : i + 1, cols] += d_taps[i]
        d_rate_ref[h : h + 1, :] += jnp.broadcast_to(d_rate, (1, 128))
        d_onorm_ref[h : h + 1, :] += d_onorm
        d_gates = d_gates + jnp.where(lane == 2 * h, jnp.broadcast_to(d_alpha, lane.shape), 0.0)
        d_gates = d_gates + jnp.where(lane == 2 * h + 1, jnp.broadcast_to(d_beta, lane.shape), 0.0)
    d_gates_ref[...] = d_gates.astype(d_gates_ref.dtype)


def common_specs(dims, blocks, order):
    heads, mix, conv, value = dims
    ratio = BLOCK // HALO
    at = lambda s, b: s * blocks + order(b)
    return [
        pl.BlockSpec((HALO, heads * mix), lambda s, b: (jnp.maximum(at(s, b) * ratio - 1, 0), 0)),
        pl.BlockSpec((BLOCK, heads * mix), lambda s, b: (at(s, b), 0)),
        pl.BlockSpec((BLOCK, heads * 2), lambda s, b: (at(s, b), 0)),
        pl.BlockSpec((BLOCK, 8), lambda s, b: (at(s, b), 0)),
        pl.BlockSpec((4, heads * conv), lambda s, b: (0, 0)),
        pl.BlockSpec((1, heads), lambda s, b: (0, 0)),
        pl.BlockSpec((heads, value), lambda s, b: (0, 0)),
    ], at


def mixer_forward(proj, gates_pre, aux, conv2d, rate, onorm, dims, seqs, interpret=False):
    heads, mix, conv, value = dims
    key_width = (conv - value) // 2
    rows = proj.shape[0]
    blocks = rows // seqs // BLOCK
    specs, at = common_specs(dims, blocks, lambda b: b)
    return pl.pallas_call(
        functools.partial(forward_kernel, dims),
        grid=(seqs, blocks),
        in_specs=specs,
        out_specs=[
            pl.BlockSpec((BLOCK, heads * value), lambda s, b: (at(s, b), 0)),
            pl.BlockSpec((1, heads * key_width, value), lambda s, b: (at(s, b), 0, 0)),
            pl.BlockSpec((1, heads * BLOCK, BLOCK), lambda s, b: (at(s, b), 0, 0)),
        ],
        out_shape=[
            jax.ShapeDtypeStruct((rows, heads * value), jnp.bfloat16),
            jax.ShapeDtypeStruct((seqs * blocks, heads * key_width, value), jnp.float32),
            jax.ShapeDtypeStruct((seqs * blocks, heads * BLOCK, BLOCK), jnp.float32),
        ],
        scratch_shapes=[pltpu.VMEM((heads * key_width, value), jnp.float32)],
        cost_estimate=pl.CostEstimate(flops=rows * heads * 2000000, bytes_accessed=rows * heads * 8192, transcendentals=0),
        name="mixer_forward",
        interpret=interpret,
    )(proj, proj, gates_pre, aux, conv2d, rate, onorm)


def mixer_backward(proj, gates_pre, aux, conv2d, rate, onorm, states, inverses, d_heads, dims, seqs, interpret=False):
    heads, mix, conv, value = dims
    key_width = (conv - value) // 2
    rows = proj.shape[0]
    blocks = rows // seqs // BLOCK
    specs, at = common_specs(dims, blocks, lambda b: blocks - 1 - b)
    return pl.pallas_call(
        functools.partial(backward_kernel, dims),
        grid=(seqs, blocks),
        in_specs=specs + [
            pl.BlockSpec((1, heads * key_width, value), lambda s, b: (at(s, b), 0, 0)),
            pl.BlockSpec((1, heads * BLOCK, BLOCK), lambda s, b: (at(s, b), 0, 0)),
            pl.BlockSpec((BLOCK, heads * value), lambda s, b: (at(s, b), 0)),
        ],
        out_specs=[
            pl.BlockSpec((BLOCK, heads * mix), lambda s, b: (at(s, b), 0)),
            pl.BlockSpec((BLOCK, heads * 2), lambda s, b: (at(s, b), 0)),
            pl.BlockSpec((4, heads * conv), lambda s, b: (0, 0)),
            pl.BlockSpec((heads, 128), lambda s, b: (0, 0)),
            pl.BlockSpec((heads, value), lambda s, b: (0, 0)),
        ],
        out_shape=[
            jax.ShapeDtypeStruct((rows, heads * mix), jnp.bfloat16),
            jax.ShapeDtypeStruct((rows, heads * 2), jnp.bfloat16),
            jax.ShapeDtypeStruct((4, heads * conv), jnp.float32),
            jax.ShapeDtypeStruct((heads, 128), jnp.float32),
            jax.ShapeDtypeStruct((heads, value), jnp.float32),
        ],
        scratch_shapes=[
            pltpu.VMEM((heads * key_width, value), jnp.float32),
            pltpu.VMEM((HALO, heads * conv), jnp.float32),
        ],
        cost_estimate=pl.CostEstimate(flops=rows * heads * 5000000, bytes_accessed=rows * heads * 12288, transcendentals=0),
        name="mixer_backward",
        interpret=interpret,
    )(proj, proj, gates_pre, aux, conv2d, rate, onorm, states, inverses, d_heads)


def swish_gate(gate, up):
    return jax.nn.silu(gate) * up


def local(
    tokens,
    seg_starts,
    norm1_gain,
    w_mix,
    w_gates,
    conv_w,
    decay_rate,
    onorm_gain,
    w_out,
    norm2_gain,
    w_gu,
    w_down,
    cotangent,
):
    f32 = jnp.float32
    bf16 = jnp.bfloat16
    local_rows, width = tokens.shape
    seqs = seg_starts.shape[0]
    heads = w_mix.shape[1]
    mix_cols = w_mix.shape[2]
    value_width = onorm_gain.shape[1]
    hidden = w_down.shape[0]
    mix2d = w_mix.reshape(width, heads * mix_cols)
    gates2d = w_gates.reshape(width, heads * 2)
    out2d = w_out.reshape(heads * value_width, width)
    gu2d = w_gu.reshape(width, 2 * hidden)
    resid = tokens.astype(f32)
    normed1 = rms_norm(resid, norm1_gain).astype(bf16)
    rows1 = lax.all_gather(normed1, "tensor", axis=0, tiled=True)
    total_rows = rows1.shape[0]
    length = total_rows // seqs
    dims = (heads, mix_cols, conv_w.shape[2], value_width)
    proj = jnp.dot(rows1, mix2d, preferred_element_type=f32)
    gates_pre = jnp.dot(rows1, gates2d, preferred_element_type=f32)
    aux = jax.vmap(segment_ids, in_axes=(0, None))(seg_starts, length).reshape(total_rows, 8)
    mixer_args = (proj, gates_pre, aux, conv_w.reshape(4, -1), decay_rate[None, :], onorm_gain)
    mixed, states, inverses = mixer_forward(*mixer_args, dims, seqs)
    cot_rows = lax.all_gather(cotangent, "tensor", axis=0, tiled=True)
    mixed, cot_rows = lax.optimization_barrier((mixed, cot_rows))
    resid2 = resid + lax.psum_scatter(
        jnp.dot(mixed, out2d, preferred_element_type=f32).astype(jnp.bfloat16),
        "tensor",
        scatter_dimension=0,
        tiled=True,
    ).astype(jnp.float32)
    normed2 = rms_norm(resid2, norm2_gain).astype(bf16)
    rows2 = lax.all_gather(normed2, "tensor", axis=0, tiled=True)
    gu = jnp.dot(rows2, gu2d, preferred_element_type=f32).reshape(total_rows, 2, hidden)
    act = swish_gate(gu[:, 0], gu[:, 1]).astype(bf16)
    ffn_part = jnp.dot(act, w_down, preferred_element_type=f32).astype(bf16)
    grad_down = jnp.dot(cot_rows.T, act, preferred_element_type=f32).astype(bf16)
    d_act = jnp.dot(cot_rows, w_down.T, preferred_element_type=f32)
    _, swish_back = jax.vjp(swish_gate, gu[:, 0], gu[:, 1])
    d_gate, d_up = swish_back(d_act)
    d_gu = jnp.stack([d_gate, d_up], axis=1).astype(bf16).reshape(total_rows, 2 * hidden)
    grad_gu = jnp.dot(rows2.T, d_gu, preferred_element_type=f32).astype(bf16)
    d_normed2 = lax.psum_scatter(
        jnp.dot(d_gu, gu2d.T, preferred_element_type=f32).astype(jnp.bfloat16),
        "tensor",
        scatter_dimension=0,
        tiled=True,
    ).astype(jnp.float32)
    _, norm2_back = jax.vjp(rms_norm, resid2, norm2_gain)
    d_resid_ffn, gain2_part = norm2_back(d_normed2)
    d_resid2 = cotangent.astype(f32) + d_resid_ffn
    d_rows = lax.all_gather(d_resid2.astype(bf16), "tensor", axis=0, tiled=True)
    grad_out = jnp.dot(d_rows.T, mixed, preferred_element_type=f32).astype(bf16)
    d_heads = jnp.dot(d_rows, out2d.T, preferred_element_type=f32)
    d_heads, ffn_part = lax.optimization_barrier((d_heads, ffn_part))
    ffn_sum = lax.psum_scatter(ffn_part, "tensor", scatter_dimension=0, tiled=True)
    d_proj_b, d_gates_b, d_conv, d_rate, d_onorm = mixer_backward(
        *mixer_args, states, inverses, d_heads, dims, seqs
    )
    d_proj_b, ffn_sum = lax.optimization_barrier((d_proj_b, ffn_sum))
    output = (resid2 + ffn_sum.astype(f32)).astype(bf16)
    d_conv = d_conv.reshape(conv_w.shape)
    d_rate = d_rate[:, 0]
    grad_mix = jnp.dot(rows1.T, d_proj_b, preferred_element_type=f32).astype(bf16)
    grad_gates = jnp.dot(rows1.T, d_gates_b, preferred_element_type=f32).astype(bf16)
    d_normed1 = lax.psum_scatter(
        (
            jnp.dot(d_proj_b, mix2d.T, preferred_element_type=f32)
            + jnp.dot(d_gates_b, gates2d.T, preferred_element_type=f32)
        ).astype(jnp.bfloat16),
        "tensor",
        scatter_dimension=0,
        tiled=True,
    ).astype(jnp.float32)
    d_normed1, grad_mix = lax.optimization_barrier((d_normed1, grad_mix))
    _, norm1_back = jax.vjp(rms_norm, resid, norm1_gain)
    d_resid1, gain1_part = norm1_back(d_normed1)
    grad_tokens = (d_resid2 + d_resid1).astype(bf16)
    grad_conv, grad_rate, grad_onorm = lax.psum((d_conv, d_rate, d_onorm), "dp")
    pad = -(2 * heads) % 128
    grads = jnp.concatenate(
        [grad_mix, grad_gu, grad_down, grad_out, jnp.pad(grad_gates, ((0, 0), (0, pad)))], axis=1
    )
    shares = lax.psum_scatter(grads, "dp", scatter_dimension=0, tiled=True).astype(f32)
    cuts = []
    place = 0
    for size in (heads * mix_cols, 2 * hidden, hidden, heads * value_width, 2 * heads):
        cuts.append(shares[:, place : place + size])
        place += size
    mix_share = cuts[0].reshape(-1, heads, mix_cols)
    gu_share = cuts[1].reshape(-1, 2, hidden)
    down_share = cuts[2].T
    out_share = cuts[3].T.reshape(heads, value_width, -1)
    gates_share = cuts[4].reshape(-1, heads, 2)
    gain1_share = lax.psum_scatter(gain1_part, "dp", scatter_dimension=0, tiled=True)
    gain2_share = lax.psum_scatter(gain2_part, "dp", scatter_dimension=0, tiled=True)
    gain1_total, gain2_total = lax.psum((gain1_share, gain2_share), "tensor")
    return (
        output,
        grad_tokens,
        gain1_total,
        mix_share,
        gates_share,
        grad_conv,
        grad_rate,
        grad_onorm,
        out_share,
        gain2_total,
        gu_share,
        down_share,
    )


def solution(mesh):
    in_specs = (
        P(("dp", "tensor"), None),
        P("dp", None),
        P(),
        P(None, "tensor", None),
        P(None, "tensor", None),
        P(None, "tensor", None),
        P("tensor"),
        P("tensor", None),
        P("tensor", None, None),
        P(),
        P(None, None, "tensor"),
        P("tensor", None),
        P(("dp", "tensor"), None),
    )
    out_specs = (
        P(("dp", "tensor"), None),
        P(("dp", "tensor"), None),
        P("dp"),
        P("dp", "tensor", None),
        P("dp", "tensor", None),
        P(None, "tensor", None),
        P("tensor"),
        P("tensor", None),
        P("tensor", None, "dp"),
        P("dp"),
        P("dp", None, "tensor"),
        P("tensor", "dp"),
    )
    return jax.shard_map(local, mesh=mesh, in_specs=in_specs, out_specs=out_specs, check_vma=False)
```

```python
import functools

import jax
import jax.numpy as jnp
from jax import lax
from jax.experimental import pallas as pl
from jax.experimental.pallas import tpu as pltpu
from jax.sharding import PartitionSpec as P

BLOCK = 64
HALO = 8
HI = lax.Precision.HIGHEST


def contract(a, b, dims, exact=False):
    if exact:
        return lax.dot_general(a, b, (dims, ((), ())), precision=HI, preferred_element_type=jnp.float32)
    a, b = a.astype(jnp.bfloat16), b.astype(jnp.bfloat16)
    return lax.dot_general(a, b, (dims, ((), ())), preferred_element_type=jnp.float32)


NN, NT, TN = ((1,), (0,)), ((1,), (1,)), ((0,), (0,))


@functools.partial(jax.custom_vjp, nondiff_argnums=(2,))
def mm_nn(a, b, exact=False):
    return contract(a, b, NN, exact)


mm_nn.defvjp(
    lambda a, b, exact: (contract(a, b, NN, exact), (a, b)),
    lambda exact, res, g: (contract(g, res[1], NT, exact), contract(res[0], g, TN, exact)),
)


@functools.partial(jax.custom_vjp, nondiff_argnums=(2,))
def mm_nt(a, b, exact=False):
    return contract(a, b, NT, exact)


mm_nt.defvjp(
    lambda a, b, exact: (contract(a, b, NT, exact), (a, b)),
    lambda exact, res, g: (contract(g, res[1], NN, exact), contract(g, res[0], TN, exact)),
)


@functools.partial(jax.custom_vjp, nondiff_argnums=(2,))
def mm_tn(a, b, exact=False):
    return contract(a, b, TN, exact)


mm_tn.defvjp(
    lambda a, b, exact: (contract(a, b, TN, exact), (a, b)),
    lambda exact, res, g: (contract(res[1], g, NT, exact), contract(res[0], g, NN, exact)),
)


@jax.custom_vjp
def solve(lower, rhs, inverse):
    return contract(inverse, rhs, NN)


def solve_fwd(lower, rhs, inverse):
    errs = contract(inverse, rhs, NN)
    return errs, (inverse, errs)


def solve_bwd(res, g):
    inverse, errs = res
    d_rhs = contract(inverse, g, TN)
    return -contract(d_rhs, errs, NT), d_rhs, jnp.zeros_like(inverse)


solve.defvjp(solve_fwd, solve_bwd)


@functools.partial(jax.custom_vjp, nondiff_argnums=(1,))
def keepsum(x, axis):
    return jnp.sum(x, axis=axis, keepdims=True)


keepsum.defvjp(
    lambda x, axis: (jnp.sum(x, axis=axis, keepdims=True), x),
    lambda axis, x, g: (jnp.broadcast_to(g, x.shape),),
)


@functools.partial(jax.custom_vjp, nondiff_argnums=(1,))
def spread(x, shape):
    return jnp.broadcast_to(x, shape)


def spread_bwd(shape, x, g):
    for axis in range(2):
        if x.shape[axis] == 1 and shape[axis] != 1:
            g = jnp.sum(g, axis=axis, keepdims=True)
    return (g,)


spread.defvjp(lambda x, shape: (jnp.broadcast_to(x, shape), x), spread_bwd)


@functools.partial(jax.custom_vjp, nondiff_argnums=(1,))
def lagged(ext, lag):
    return pltpu.roll(ext, lag, 0)[HALO:] if lag else ext[HALO:]


def lagged_bwd(lag, ext, g):
    full = jnp.concatenate([jnp.zeros((HALO, g.shape[1]), g.dtype), g], axis=0)
    return (pltpu.roll(full, full.shape[0] - lag, 0) if lag else full,)


lagged.defvjp(lambda ext, lag: (lagged(ext, lag), ext), lagged_bwd)


@jax.custom_vjp
def softplus(x):
    return jnp.maximum(x, 0.0) + jnp.log1p(jnp.exp(-jnp.abs(x)))


softplus.defvjp(lambda x: (softplus(x), x), lambda x, g: (g * jax.nn.sigmoid(x),))


def silu(x):
    return x * jax.nn.sigmoid(x)


def rms_norm(rows, gain):
    return rows * lax.rsqrt(jnp.mean(rows * rows, axis=-1, keepdims=True) + 1e-06) * gain


def segment_ids(starts_row, length):
    places = jnp.arange(length, dtype=jnp.int32)
    flags = jnp.any(starts_row[:, None] == places[None, :], axis=0).astype(jnp.int32)
    seg = jnp.cumsum(flags)
    before = jnp.concatenate([seg[:1], seg[:-1]])
    columns = [seg]
    for lag in range(1, 4):
        moved = jnp.pad(seg, (lag, 0), constant_values=-1)[:length]
        columns.append(moved == seg)
    columns.append(seg == jnp.repeat(before[::BLOCK], BLOCK))
    columns += [jnp.zeros_like(seg)] * 3
    return jnp.stack([c.astype(jnp.float32) for c in columns], axis=1)


def masks():
    shape = (BLOCK, BLOCK)
    row = lax.broadcasted_iota(jnp.int32, shape, 0)
    col = lax.broadcasted_iota(jnp.int32, shape, 1)
    return row, col


def unit_inverse(lowers):
    row, col = masks()
    out = None
    size = 0
    while (1 << size) < BLOCK:
        part = jnp.logical_and(
            (row >> (size + 1)) == (col >> (size + 1)),
            jnp.logical_and(((row >> size) & 1) == 1, ((col >> size) & 1) == 0),
        )
        cut = [jnp.where(part, low, 0.0) for low in lowers]
        if out is None:
            unit = (row == col).astype(jnp.float32)
            out = [unit - c for c in cut]
        else:
            mid = [contract(c, t, NN, True) for c, t in zip(cut, out)]
            out = [t - contract(t, m, NN, True) for t, m in zip(out, mid)]
        size += 1
    return out


def front(ext, alpha_pre, beta_pre, taps, rate, aux, key_width):
    rows = BLOCK
    wide = (rows, ext.shape[1])
    square = (BLOCK, BLOCK)
    total = spread(taps[3], wide) * lagged(ext, 0)
    for lag in range(1, 4):
        keep = jnp.broadcast_to(aux[lag], wide)
        total = total + spread(taps[3 - lag], wide) * (lagged(ext, lag) * keep)
    act = silu(total)

    def unit_rows(x):
        return x * spread(lax.rsqrt(keepsum(x * x, 1) + 1e-06), x.shape)

    return act, unit_rows


def block_terms(query, keys, beta_pre, alpha_pre, rate, aux):
    square = (BLOCK, BLOCK)
    row, col = masks()
    eye = (row == col).astype(jnp.float32)
    seg_col = jnp.broadcast_to(aux[0], square)
    seg_row = jnp.broadcast_to(jnp.sum(eye * seg_col, axis=0, keepdims=True), square)
    live = jnp.logical_and(seg_col == seg_row, row >= col)
    beta = jax.nn.sigmoid(beta_pre)
    logd = -spread(rate, alpha_pre.shape) * softplus(alpha_pre)
    incl = (row >= col).astype(jnp.float32)
    logd_row = keepsum(eye * spread(logd, square), 0)
    cum = keepsum(incl * spread(logd_row, square), 1)
    cum_row = keepsum(eye * spread(cum, square), 0)
    diff = spread(cum, square) - spread(cum_row, square)
    within = jnp.where(live, jnp.exp(jnp.where(live, diff, 0.0)), 0.0)
    carried = jnp.exp(cum) * aux[4]
    kk = mm_nt(keys, keys, True)
    strict = (row > col).astype(jnp.float32)
    lower = spread(beta, square) * within * kk * strict
    place = lax.broadcasted_iota(jnp.int32, (BLOCK, 1), 0)
    last = (place == BLOCK - 1).astype(jnp.float32)
    cum_last = spread(keepsum(cum * last, 0), cum.shape)
    seg_last = jnp.broadcast_to(jnp.sum(aux[0] * last, axis=0, keepdims=True), cum.shape)
    same = seg_last == aux[0]
    final = jnp.where(same, jnp.exp(jnp.where(same, cum_last - cum, 0.0)), 0.0)
    carried_last = keepsum(carried * last, 0)
    return beta, within, carried, lower, final, carried_last


def split_heads(ext, taps, aux, key_width):
    act, unit_rows = front(ext, None, None, taps, None, aux, key_width)
    query = unit_rows(act[:, :key_width]) * key_width ** (-0.5)
    keys = unit_rows(act[:, key_width : 2 * key_width])
    return query, keys, act[:, 2 * key_width :]


def advance(query, keys, values, terms, state, inverse, gate_out, onorm):
    beta, within, carried, lower, final, carried_last = terms
    tall = values.shape
    rhs = spread(beta, tall) * (values - spread(carried, tall) * mm_nn(keys, state))
    errs = solve(lower, rhs, inverse)
    read = spread(carried, tall) * mm_nn(query, state)
    read = read + mm_nn(within * mm_nt(query, keys), errs)
    new_state = spread(carried_last, state.shape) * state
    new_state = new_state + mm_tn(spread(final, keys.shape) * keys, errs)
    scale = lax.rsqrt(keepsum(read * read, 1) * (1.0 / tall[1]) + 1e-05)
    out = read * spread(scale, tall) * spread(onorm, tall) * silu(gate_out)
    return out, new_state


def head_inputs(h, dims, halo_ref, proj_ref, gates_ref, conv_ref, rate_ref, onorm_ref):
    heads, mix, conv, value = dims
    base = h * mix
    ext = jnp.concatenate(
        [halo_ref[:, base : base + conv], proj_ref[:, base : base + conv]], axis=0
    )
    gate_out = proj_ref[:, base + conv : base + mix]
    alpha_pre = gates_ref[:, 2 * h : 2 * h + 1]
    beta_pre = gates_ref[:, 2 * h + 1 : 2 * h + 2]
    taps = tuple(conv_ref[i : i + 1, h * conv : (h + 1) * conv] for i in range(4))
    rate = rate_ref[:, h : h + 1]
    onorm = onorm_ref[h : h + 1, :]
    return ext, gate_out, alpha_pre, beta_pre, taps, rate, onorm


def forward_kernel(dims, halo_ref, proj_ref, gates_ref, aux_ref, conv_ref, rate_ref, onorm_ref,
                   out_ref, states_ref, inv_ref, state):
    heads, mix, conv, value = dims
    key_width = (conv - value) // 2

    @pl.when(pl.program_id(1) == 0)
    def _():
        state[...] = jnp.zeros_like(state)

    aux = [aux_ref[:, i : i + 1] for i in range(5)]
    work = []
    for h in range(heads):
        ext, gate_out, alpha_pre, beta_pre, taps, rate, onorm = head_inputs(
            h, dims, halo_ref, proj_ref, gates_ref, conv_ref, rate_ref, onorm_ref
        )
        query, keys, values = split_heads(ext, taps, aux, key_width)
        terms = block_terms(query, keys, beta_pre, alpha_pre, rate, aux)
        work.append((query, keys, values, terms, gate_out, onorm))
    inverses = unit_inverse([w[3][3] for w in work])
    for h in range(heads):
        query, keys, values, terms, gate_out, onorm = work[h]
        old = state[h * key_width : (h + 1) * key_width, :]
        out, new = advance(query, keys, values, terms, old, inverses[h], gate_out, onorm)
        states_ref[0, h * key_width : (h + 1) * key_width, :] = old
        state[h * key_width : (h + 1) * key_width, :] = new
        inv_ref[0, h * BLOCK : (h + 1) * BLOCK, :] = inverses[h]
        out_ref[:, h * value : (h + 1) * value] = out.astype(out_ref.dtype)


def backward_kernel(dims, halo_ref, proj_ref, gates_ref, aux_ref, conv_ref, rate_ref, onorm_ref,
                    states_ref, inv_ref, d_out_ref,
                    d_proj_ref, d_gates_ref, d_conv_ref, d_rate_ref, d_onorm_ref, d_state, spill):
    heads, mix, conv, value = dims
    key_width = (conv - value) // 2

    @pl.when(pl.program_id(1) == 0)
    def _():
        d_state[...] = jnp.zeros_like(d_state)
        spill[...] = jnp.zeros_like(spill)

    @pl.when(jnp.logical_and(pl.program_id(0) == 0, pl.program_id(1) == 0))
    def _():
        d_conv_ref[...] = jnp.zeros_like(d_conv_ref)
        d_rate_ref[...] = jnp.zeros_like(d_rate_ref)
        d_onorm_ref[...] = jnp.zeros_like(d_onorm_ref)

    aux = [aux_ref[:, i : i + 1] for i in range(5)]
    lane = lax.broadcasted_iota(jnp.int32, (BLOCK, 2 * heads), 1)
    d_gates = jnp.zeros((BLOCK, 2 * heads), jnp.float32)
    for h in range(heads):
        ext, gate_out, alpha_pre, beta_pre, taps, rate, onorm = head_inputs(
            h, dims, halo_ref, proj_ref, gates_ref, conv_ref, rate_ref, onorm_ref
        )
        old = states_ref[0, h * key_width : (h + 1) * key_width, :]
        inverse = inv_ref[0, h * BLOCK : (h + 1) * BLOCK, :]

        act, act_back = jax.vjp(
            lambda e, t: front(e, None, None, t, None, aux, key_width)[0], ext, taps
        )
        raw_q = act[:, :key_width]
        raw_k = act[:, key_width : 2 * key_width]
        values = act[:, 2 * key_width :]

        def rest(raw_q, raw_k, values, gate_out, alpha_pre, beta_pre, rate, onorm, old):
            def unit_rows(x):
                return x * spread(lax.rsqrt(keepsum(x * x, 1) + 1e-06), x.shape)

            query = unit_rows(raw_q) * key_width ** (-0.5)
            keys = unit_rows(raw_k)
            terms = block_terms(query, keys, beta_pre, alpha_pre, rate, aux)
            return advance(query, keys, values, terms, old, inverse, gate_out, onorm)

        _, back = jax.vjp(
            rest, raw_q, raw_k, values, gate_out, alpha_pre, beta_pre, rate, onorm, old
        )
        d_out = d_out_ref[:, h * value : (h + 1) * value]
        span = slice(h * key_width, (h + 1) * key_width)
        d_q, d_k, d_v, d_gate, d_alpha, d_beta, d_rate, d_onorm, d_old = back(
            (d_out, d_state[span, :])
        )
        d_state[span, :] = d_old
        d_ext, d_taps = act_back(jnp.concatenate([d_q, d_k, d_v], axis=1))
        cols = slice(h * conv, (h + 1) * conv)
        carry = jnp.concatenate(
            [jnp.zeros((BLOCK - HALO, conv), jnp.float32), spill[:, cols]], axis=0
        )
        d_mixed = d_ext[HALO:] + carry
        spill[:, cols] = d_ext[:HALO]
        base = h * mix
        d_proj_ref[:, base : base + conv] = d_mixed.astype(d_proj_ref.dtype)
        d_proj_ref[:, base + conv : base + mix] = d_gate.astype(d_proj_ref.dtype)
        for i in range(4):
            d_conv_ref[i : i + 1, cols] += d_taps[i]
        d_rate_ref[h : h + 1, :] += jnp.broadcast_to(d_rate, (1, 128))
        d_onorm_ref[h : h + 1, :] += d_onorm
        d_gates = d_gates + jnp.where(lane == 2 * h, jnp.broadcast_to(d_alpha, lane.shape), 0.0)
        d_gates = d_gates + jnp.where(lane == 2 * h + 1, jnp.broadcast_to(d_beta, lane.shape), 0.0)
    d_gates_ref[...] = d_gates.astype(d_gates_ref.dtype)


def common_specs(dims, blocks, order):
    heads, mix, conv, value = dims
    ratio = BLOCK // HALO
    at = lambda s, b: s * blocks + order(b)
    return [
        pl.BlockSpec((HALO, heads * mix), lambda s, b: (jnp.maximum(at(s, b) * ratio - 1, 0), 0)),
        pl.BlockSpec((BLOCK, heads * mix), lambda s, b: (at(s, b), 0)),
        pl.BlockSpec((BLOCK, heads * 2), lambda s, b: (at(s, b), 0)),
        pl.BlockSpec((BLOCK, 8), lambda s, b: (at(s, b), 0)),
        pl.BlockSpec((4, heads * conv), lambda s, b: (0, 0)),
        pl.BlockSpec((1, heads), lambda s, b: (0, 0)),
        pl.BlockSpec((heads, value), lambda s, b: (0, 0)),
    ], at


def mixer_forward(proj, gates_pre, aux, conv2d, rate, onorm, dims, seqs, interpret=False):
    heads, mix, conv, value = dims
    key_width = (conv - value) // 2
    rows = proj.shape[0]
    blocks = rows // seqs // BLOCK
    specs, at = common_specs(dims, blocks, lambda b: b)
    return pl.pallas_call(
        functools.partial(forward_kernel, dims),
        grid=(seqs, blocks),
        in_specs=specs,
        out_specs=[
            pl.BlockSpec((BLOCK, heads * value), lambda s, b: (at(s, b), 0)),
            pl.BlockSpec((1, heads * key_width, value), lambda s, b: (at(s, b), 0, 0)),
            pl.BlockSpec((1, heads * BLOCK, BLOCK), lambda s, b: (at(s, b), 0, 0)),
        ],
        out_shape=[
            jax.ShapeDtypeStruct((rows, heads * value), jnp.bfloat16),
            jax.ShapeDtypeStruct((seqs * blocks, heads * key_width, value), jnp.float32),
            jax.ShapeDtypeStruct((seqs * blocks, heads * BLOCK, BLOCK), jnp.float32),
        ],
        scratch_shapes=[pltpu.VMEM((heads * key_width, value), jnp.float32)],
        cost_estimate=pl.CostEstimate(flops=rows * heads * 2000000, bytes_accessed=rows * heads * 8192, transcendentals=0),
        name="mixer_forward",
        interpret=interpret,
    )(proj, proj, gates_pre, aux, conv2d, rate, onorm)


def mixer_backward(proj, gates_pre, aux, conv2d, rate, onorm, states, inverses, d_heads, dims, seqs, interpret=False):
    heads, mix, conv, value = dims
    key_width = (conv - value) // 2
    rows = proj.shape[0]
    blocks = rows // seqs // BLOCK
    specs, at = common_specs(dims, blocks, lambda b: blocks - 1 - b)
    return pl.pallas_call(
        functools.partial(backward_kernel, dims),
        grid=(seqs, blocks),
        in_specs=specs + [
            pl.BlockSpec((1, heads * key_width, value), lambda s, b: (at(s, b), 0, 0)),
            pl.BlockSpec((1, heads * BLOCK, BLOCK), lambda s, b: (at(s, b), 0, 0)),
            pl.BlockSpec((BLOCK, heads * value), lambda s, b: (at(s, b), 0)),
        ],
        out_specs=[
            pl.BlockSpec((BLOCK, heads * mix), lambda s, b: (at(s, b), 0)),
            pl.BlockSpec((BLOCK, heads * 2), lambda s, b: (at(s, b), 0)),
            pl.BlockSpec((4, heads * conv), lambda s, b: (0, 0)),
            pl.BlockSpec((heads, 128), lambda s, b: (0, 0)),
            pl.BlockSpec((heads, value), lambda s, b: (0, 0)),
        ],
        out_shape=[
            jax.ShapeDtypeStruct((rows, heads * mix), jnp.bfloat16),
            jax.ShapeDtypeStruct((rows, heads * 2), jnp.bfloat16),
            jax.ShapeDtypeStruct((4, heads * conv), jnp.float32),
            jax.ShapeDtypeStruct((heads, 128), jnp.float32),
            jax.ShapeDtypeStruct((heads, value), jnp.float32),
        ],
        scratch_shapes=[
            pltpu.VMEM((heads * key_width, value), jnp.float32),
            pltpu.VMEM((HALO, heads * conv), jnp.float32),
        ],
        cost_estimate=pl.CostEstimate(flops=rows * heads * 5000000, bytes_accessed=rows * heads * 12288, transcendentals=0),
        name="mixer_backward",
        interpret=interpret,
    )(proj, proj, gates_pre, aux, conv2d, rate, onorm, states, inverses, d_heads)


def swish_gate(gate, up):
    return jax.nn.silu(gate) * up


def local(
    tokens,
    seg_starts,
    norm1_gain,
    w_mix,
    w_gates,
    conv_w,
    decay_rate,
    onorm_gain,
    w_out,
    norm2_gain,
    w_gu,
    w_down,
    cotangent,
):
    f32 = jnp.float32
    bf16 = jnp.bfloat16
    local_rows, width = tokens.shape
    seqs = seg_starts.shape[0]
    heads = w_mix.shape[1]
    mix_cols = w_mix.shape[2]
    value_width = onorm_gain.shape[1]
    hidden = w_down.shape[0]
    mix2d = w_mix.reshape(width, heads * mix_cols)
    gates2d = w_gates.reshape(width, heads * 2)
    out2d = w_out.reshape(heads * value_width, width)
    gu2d = w_gu.reshape(width, 2 * hidden)
    resid = tokens.astype(f32)
    normed1 = rms_norm(resid, norm1_gain).astype(bf16)
    rows1 = lax.all_gather(normed1, "tensor", axis=0, tiled=True)
    total_rows = rows1.shape[0]
    length = total_rows // seqs
    dims = (heads, mix_cols, conv_w.shape[2], value_width)
    proj = jnp.dot(rows1, mix2d, preferred_element_type=f32)
    gates_pre = jnp.dot(rows1, gates2d, preferred_element_type=f32)
    aux = jax.vmap(segment_ids, in_axes=(0, None))(seg_starts, length).reshape(total_rows, 8)
    mixer_args = (proj, gates_pre, aux, conv_w.reshape(4, -1), decay_rate[None, :], onorm_gain)
    mixed, states, inverses = mixer_forward(*mixer_args, dims, seqs)
    cot_rows = lax.all_gather(cotangent, "tensor", axis=0, tiled=True)
    mixed, cot_rows = lax.optimization_barrier((mixed, cot_rows))
    resid2 = resid + lax.psum_scatter(
        jnp.dot(mixed, out2d, preferred_element_type=f32).astype(jnp.bfloat16),
        "tensor",
        scatter_dimension=0,
        tiled=True,
    ).astype(jnp.float32)
    normed2 = rms_norm(resid2, norm2_gain).astype(bf16)
    rows2 = lax.all_gather(normed2, "tensor", axis=0, tiled=True)
    gu = jnp.dot(rows2, gu2d, preferred_element_type=f32).reshape(total_rows, 2, hidden)
    act = swish_gate(gu[:, 0], gu[:, 1]).astype(bf16)
    ffn_part = jnp.dot(act, w_down, preferred_element_type=f32).astype(bf16)
    grad_down = jnp.dot(cot_rows.T, act, preferred_element_type=f32).astype(bf16)
    d_act = jnp.dot(cot_rows, w_down.T, preferred_element_type=f32)
    _, swish_back = jax.vjp(swish_gate, gu[:, 0], gu[:, 1])
    d_gate, d_up = swish_back(d_act)
    d_gu = jnp.stack([d_gate, d_up], axis=1).astype(bf16).reshape(total_rows, 2 * hidden)
    grad_gu = jnp.dot(rows2.T, d_gu, preferred_element_type=f32).astype(bf16)
    d_normed2 = lax.psum_scatter(
        jnp.dot(d_gu, gu2d.T, preferred_element_type=f32).astype(jnp.bfloat16),
        "tensor",
        scatter_dimension=0,
        tiled=True,
    ).astype(jnp.float32)
    _, norm2_back = jax.vjp(rms_norm, resid2, norm2_gain)
    d_resid_ffn, gain2_part = norm2_back(d_normed2)
    d_resid2 = cotangent.astype(f32) + d_resid_ffn
    d_rows = lax.all_gather(d_resid2.astype(bf16), "tensor", axis=0, tiled=True)
    grad_out = jnp.dot(d_rows.T, mixed, preferred_element_type=f32).astype(bf16)
    d_heads = jnp.dot(d_rows, out2d.T, preferred_element_type=f32)
    d_heads, ffn_part = lax.optimization_barrier((d_heads, ffn_part))
    ffn_sum = lax.psum_scatter(ffn_part, "tensor", scatter_dimension=0, tiled=True)
    d_proj_b, d_gates_b, d_conv, d_rate, d_onorm = mixer_backward(
        *mixer_args, states, inverses, d_heads, dims, seqs
    )
    d_proj_b, ffn_sum = lax.optimization_barrier((d_proj_b, ffn_sum))
    output = (resid2 + ffn_sum.astype(f32)).astype(bf16)
    d_conv = d_conv.reshape(conv_w.shape)
    d_rate = d_rate[:, 0]
    grad_mix = jnp.dot(rows1.T, d_proj_b, preferred_element_type=f32).astype(bf16)
    grad_gates = jnp.dot(rows1.T, d_gates_b, preferred_element_type=f32).astype(bf16)
    d_normed1 = lax.psum_scatter(
        (
            jnp.dot(d_proj_b, mix2d.T, preferred_element_type=f32)
            + jnp.dot(d_gates_b, gates2d.T, preferred_element_type=f32)
        ).astype(jnp.bfloat16),
        "tensor",
        scatter_dimension=0,
        tiled=True,
    ).astype(jnp.float32)
    pad = -(2 * heads) % 128
    grads = jnp.concatenate(
        [grad_mix, grad_gu, grad_down, grad_out, jnp.pad(grad_gates, ((0, 0), (0, pad)))], axis=1
    )
    d_normed1, grads = lax.optimization_barrier((d_normed1, grads))
    _, norm1_back = jax.vjp(rms_norm, resid, norm1_gain)
    d_resid1, gain1_part = norm1_back(d_normed1)
    grad_tokens = (d_resid2 + d_resid1).astype(bf16)
    grad_conv, grad_rate, grad_onorm = lax.psum((d_conv, d_rate, d_onorm), "dp")
    shares = lax.psum_scatter(grads, "dp", scatter_dimension=0, tiled=True).astype(f32)
    cuts = []
    place = 0
    for size in (heads * mix_cols, 2 * hidden, hidden, heads * value_width, 2 * heads):
        cuts.append(shares[:, place : place + size])
        place += size
    mix_share = cuts[0].reshape(-1, heads, mix_cols)
    gu_share = cuts[1].reshape(-1, 2, hidden)
    down_share = cuts[2].T
    out_share = cuts[3].T.reshape(heads, value_width, -1)
    gates_share = cuts[4].reshape(-1, heads, 2)
    gain1_share = lax.psum_scatter(gain1_part, "dp", scatter_dimension=0, tiled=True)
    gain2_share = lax.psum_scatter(gain2_part, "dp", scatter_dimension=0, tiled=True)
    gain1_total, gain2_total = lax.psum((gain1_share, gain2_share), "tensor")
    return (
        output,
        grad_tokens,
        gain1_total,
        mix_share,
        gates_share,
        grad_conv,
        grad_rate,
        grad_onorm,
        out_share,
        gain2_total,
        gu_share,
        down_share,
    )


def solution(mesh):
    in_specs = (
        P(("dp", "tensor"), None),
        P("dp", None),
        P(),
        P(None, "tensor", None),
        P(None, "tensor", None),
        P(None, "tensor", None),
        P("tensor"),
        P("tensor", None),
        P("tensor", None, None),
        P(),
        P(None, None, "tensor"),
        P("tensor", None),
        P(("dp", "tensor"), None),
    )
    out_specs = (
        P(("dp", "tensor"), None),
        P(("dp", "tensor"), None),
        P("dp"),
        P("dp", "tensor", None),
        P("dp", "tensor", None),
        P(None, "tensor", None),
        P("tensor"),
        P("tensor", None),
        P("tensor", None, "dp"),
        P("dp"),
        P("dp", None, "tensor"),
        P("tensor", "dp"),
    )
    return jax.shard_map(local, mesh=mesh, in_specs=in_specs, out_specs=out_specs, check_vma=False)
```
